32 devices in a mesh: rep: 8 (over y, x, core), shard: 4 (over z).
Axes of the slice: x: 2, y: 2, z: 4, core: 2. Of those that a mesh axis runs over, the one named last changes fastest.
Arguments:
- hidden: bfloat16 [8, 512, 1024], P('rep', 'shard'), may hold values from -6 to 6
- cotangent: bfloat16 [8, 512, 1024], P('rep', 'shard'), may hold values from -6 to 6
- segments: int32 [8, 512], P('rep', 'shard'), may hold values from 0 to 3, never falling along the last dimension, each value on 1 to 384 neighbouring positions
- packed: bfloat16 [1024, 3072], P('shard'), may hold values from -0.5 to 0.5
- packbias: bfloat16 [3072], P('shard'), may hold values from -3 to 3
- merger: bfloat16 [1024, 1024], P('shard'), may hold values from -0.75 to 0.75
- mergebias: bfloat16 [1024], P('shard'), may hold values from -3 to 3
- expand: bfloat16 [1024, 4096], P('shard'), may hold values from -0.1875 to 0.1875
- expandbias: bfloat16 [4096], P('shard'), may hold values from -3 to 3
- contract: bfloat16 [4096, 1024], P('shard'), may hold values from -0.09375 to 0.09375
- contractbias: bfloat16 [1024], P('shard'), may hold values from -3 to 3
- firstgain: bfloat16 [1024], P('shard'), may hold values from 0.5 to 1.5
- firstshift: bfloat16 [1024], P('shard'), may hold values from -2 to 2
- secondgain: bfloat16 [1024], P('shard'), may hold values from 0.5 to 1.5
- secondshift: bfloat16 [1024], P('shard'), may hold values from -2 to 2
Outputs:
- output: bfloat16 [8, 512, 1024], P('rep', 'shard')
- backflow: float32 [8, 512, 1024], P('rep', 'shard')
- packed_gradient: float32 [1024, 3072], P('shard')
- packbias_gradient: float32 [3072], P('shard')
- merger_gradient: float32 [1024, 1024], P('shard')
- mergebias_gradient: float32 [1024], P('shard')
- expand_gradient: float32 [1024, 4096], P('shard')
- expandbias_gradient: float32 [4096], P('shard')
- contract_gradient: float32 [4096, 1024], P('shard')
- contractbias_gradient: float32 [1024], P('shard')
- firstgain_gradient: float32 [1024], P('shard')
- firstshift_gradient: float32 [1024], P('shard')
- secondgain_gradient: float32 [1024], P('shard')
- secondshift_gradient: float32 [1024], P('shard')
The draws below stay inside these ranges and needn't reach their ends.
Inputs may be any that keep to these rules, and one draw needn't show every extreme that they name: `segments`: within a row segment numbers never fall; each document holds at least one and at most three quarters of 512 tokens, and one holds exactly that many.
All inputs are finite; a program needn't handle non-finite values.
Results may differ from the reference program's by a relative error of at most 0.019.
Values may be sent and summed in bfloat16 or wider, within the bound.
No kernel may reach another device: no remote copies, remote signals or barrier semaphores. Data moves between devices by JAX's collectives and lax.ppermute only.
A program may use at most 128 MiB of HBM per device.

```python
import math
import jax
import jax.numpy as jnp
import numpy as np
from jax import lax

D = 1024
HEADS = 16
ROT = 16
FF = 4096
DOCS = 4
LEN = 512
ROWS = 8


def draw_packed(key, part):
    first, second, third = jax.random.split(key, 3)
    query_part = jax.random.normal(first, (D, D), jnp.float32) * (2.5 / math.sqrt(D))
    value_part = jax.random.normal(third, (D, D), jnp.float32) / math.sqrt(D)
    key_part = jax.random.normal(second, (D, D), jnp.float32) / math.sqrt(D)
    joined = jnp.concatenate([query_part, key_part, value_part], axis=1)
    return jnp.clip(joined, -0.5, 0.5).astype(jnp.bfloat16)


def level_of(rng, dims, cuts, least, top_value):
    level = 1.0
    for axis_at, blocks in cuts:
        steps = jax.random.uniform(jax.random.fold_in(jax.random.fold_in(rng, 6), axis_at), (blocks,), jnp.float32, least / len(cuts), top_value / len(cuts))
        level = level * jnp.repeat(jnp.exp(steps), dims[axis_at] // blocks).reshape((-1,) + (1,) * (len(dims) - 1 - axis_at))
    return level


def split_up(number_of, total, limit, skew):
    weights = [(1 << 20) // math.isqrt(grade ** skew) + 1 for grade in range(2, number_of + 1)]
    rest, holding = total - limit - (number_of - 1), [1] * (number_of - 1)
    while rest > 0:
        movable = [i for i in range(number_of - 1) if holding[i] < limit]
        pool, budget = sum([weights[i] for i in movable]), rest
        for i in movable:
            more = min(limit - holding[i], max(1, budget * weights[i] // pool), rest)
            holding[i] = holding[i] + more
            rest = rest - more
    return np.array([limit] + holding)


def ragged(key, number_of, total, most, skew):
    if number_of == 2:
        one = jax.random.randint(key, (), max(1, total - most), min(most, total - 1) + 1)
        return jnp.stack([one, total - one])
    sizes = jnp.asarray(split_up(number_of, total, most, skew), jnp.int32)
    couples = (number_of - 1) // 2
    donor, receiver = sizes[1:1 + 2 * couples:2], sizes[2:2 + 2 * couples:2]
    margin = jnp.minimum(donor - 1, most - receiver)
    passed = jax.random.randint(jax.random.fold_in(key, 1), (couples,), 0, 1 << 20) % (margin + 1)
    sizes = sizes.at[1:1 + 2 * couples:2].set(donor - passed).at[2:2 + 2 * couples:2].set(receiver + passed)
    return sizes[jax.random.permutation(jax.random.fold_in(key, 2), number_of)]


def noise(own_key, shape, scale, most, pieces=(), kind=jnp.bfloat16):
    array = jax.random.normal(own_key, shape, jnp.float32) * scale
    if len(pieces) > 0:
        array = level_of(own_key, shape, pieces, -0.22, 0.18) * array
    return jnp.clip(array, min=-most, max=most).astype(kind)


def setup_inputs(seed: int = 0) -> dict:
    arg_keys = jax.random.split(jax.random.key(seed), 16)
    return {
        "hidden": noise(arg_keys[0], (ROWS, LEN, D), 1.0, 6.0, ((0, 8), (1, 4))),
        "cotangent": noise(arg_keys[1], (ROWS, LEN, D), 1.0, 6.0, ((0, 8), (1, 4))),
        "segments": jax.vmap(lambda own: jnp.searchsorted(jnp.cumsum(ragged(own, DOCS, LEN, LEN * 3 // 4, 0)), jnp.arange(LEN), side="right"))(jax.random.split(arg_keys[2], ROWS)).reshape((ROWS, LEN)).astype(jnp.int32),
        "packed": draw_packed(jax.random.fold_in(arg_keys[15], 71), 0),
        "packbias": noise(arg_keys[4], (3 * D,), 0.5, 3.0, ((0, 4),)),
        "merger": noise(arg_keys[5], (D, D), (D // 16) ** -0.5, 0.75, ((0, 4),)),
        "mergebias": noise(arg_keys[6], (D,), 0.5, 3.0, ((0, 4),)),
        "expand": noise(arg_keys[7], (D, FF), D ** -0.5, 0.1875, ((0, 4),)),
        "expandbias": noise(arg_keys[8], (FF,), 0.5, 3.0, ((0, 4),)),
        "contract": noise(arg_keys[9], (FF, D), FF ** -0.5, 0.09375, ((0, 4),)),
        "contractbias": noise(arg_keys[10], (D,), 0.5, 3.0, ((0, 4),)),
        "firstgain": jnp.clip(1.0 + 0.1 * jax.random.normal(arg_keys[11], (D,), jnp.float32), 0.5, 1.5).astype(jnp.bfloat16),
        "firstshift": noise(arg_keys[12], (D,), 0.3, 2.0, ((0, 4),)),
        "secondgain": jnp.clip(1.0 + 0.1 * jax.random.normal(arg_keys[13], (D,), jnp.float32), 0.5, 1.5).astype(jnp.bfloat16),
        "secondshift": noise(arg_keys[14], (D,), 0.3, 2.0, ((0, 4),)),
    }


epsilon = 1e-05
rotary_base = 10000.0

def layer_norm(values_in, scaling, shifting):
    centre = values_in - lax.optimization_barrier(jnp.mean(values_in, axis=-1, keepdims=True))
    rscale = lax.rsqrt(lax.optimization_barrier(jnp.mean(centre * centre, axis=-1, keepdims=True)) + epsilon)
    normal = centre * rscale
    return (normal * scaling + shifting, normal, rscale)

def norm_back(upstream, normal, rscale, scaling):
    scaled = upstream * scaling
    inner_part = scaled - lax.optimization_barrier(jnp.mean(scaled, axis=-1, keepdims=True)) - normal * lax.optimization_barrier(jnp.mean(scaled * normal, axis=-1, keepdims=True))
    return (rscale * inner_part, lax.optimization_barrier(jnp.sum(upstream * normal, axis=0)), lax.optimization_barrier(jnp.sum(upstream, axis=0)))

def rotary_tables(position):
    half_rot = ROT // 2
    frequency = rotary_base ** (-(jnp.arange(half_rot, dtype=jnp.float32) * 2.0) / ROT)
    angles = position.astype(jnp.float32)[:, None] * frequency[None, :]
    cosine = jnp.concatenate([jnp.cos(angles), jnp.cos(angles)], axis=1)[:, None, :]
    sine = jnp.concatenate([jnp.sin(angles), jnp.sin(angles)], axis=1)[:, None, :]
    return (cosine, sine)

def rotate(tensor, cosine, sine):
    half_rot = ROT // 2
    front = tensor[..., :ROT]
    turned = jnp.concatenate([-front[..., half_rot:], front[..., :half_rot]], axis=-1)
    return jnp.concatenate([front * cosine + turned * sine, tensor[..., ROT:]], axis=-1)

def unrotate(tensor, cosine, sine):
    half_rot = ROT // 2
    front = tensor[..., :ROT]
    moved = front * sine
    turned = jnp.concatenate([moved[..., half_rot:], -moved[..., :half_rot]], axis=-1)
    return jnp.concatenate([front * cosine + turned, tensor[..., ROT:]], axis=-1)

def gelu_pair(preact):
    cumulative = 0.5 * (1.0 + jax.scipy.special.erf(preact / math.sqrt(2.0)))
    density = jnp.exp(-0.5 * preact * preact) / math.sqrt(2.0 * math.pi)
    return (preact * cumulative, cumulative + preact * density)

def row_pass(hidden_row, cotangent_row, segment_row, packed, packbias, merger, mergebias, expand, expandbias, contract, contractbias, firstgain, firstshift, secondgain, secondshift):
    length = hidden_row.shape[0]
    width = hidden_row.shape[1]
    head_dim = width // HEADS
    scale = 1.0 / math.sqrt(head_dim)
    indices = jnp.arange(length, dtype=jnp.int32)
    starts = lax.optimization_barrier(jnp.sum((segment_row[None, :] < segment_row[:, None]).astype(jnp.int32), axis=1))
    cosine, sine = rotary_tables(indices - starts)
    allowed = (segment_row[:, None] == segment_row[None, :]) & (indices[None, :] <= indices[:, None])
    hidden_f = hidden_row.astype(jnp.float32)
    gain_one = firstgain.astype(jnp.float32)
    gain_two = secondgain.astype(jnp.float32)
    normed_one, normal_one, rscale_one = layer_norm(hidden_f, gain_one, firstshift.astype(jnp.float32))
    normed_two, normal_two, rscale_two = layer_norm(hidden_f, gain_two, secondshift.astype(jnp.float32))
    normed_one = normed_one.astype(jnp.bfloat16)
    normed_two = normed_two.astype(jnp.bfloat16)
    projected = jnp.dot(normed_one, packed, preferred_element_type=jnp.float32) + packbias.astype(jnp.float32)
    queries = rotate(projected[:, :width].reshape(length, HEADS, head_dim), cosine, sine).astype(jnp.bfloat16)
    keys = rotate(projected[:, width:2 * width].reshape(length, HEADS, head_dim), cosine, sine).astype(jnp.bfloat16)
    values = projected[:, 2 * width:].reshape(length, HEADS, head_dim).astype(jnp.bfloat16)
    scores = jnp.einsum('qhd,khd->hqk', queries.astype(jnp.float32), keys.astype(jnp.float32)) * scale
    scores = jnp.where(allowed[None], scores, -1e+30)
    row_max = lax.optimization_barrier(jnp.max(scores, axis=-1, keepdims=True))
    unscaled = jnp.where(allowed[None], jnp.exp(scores - row_max), 0.0)
    row_total = lax.optimization_barrier(jnp.sum(unscaled, axis=-1, keepdims=True))
    logsum = row_max + jnp.log(row_total)
    attention = unscaled / row_total
    context = jnp.einsum('hqk,khd->qhd', attention.astype(jnp.bfloat16).astype(jnp.float32), values.astype(jnp.float32))
    context_b = context.reshape(length, width).astype(jnp.bfloat16)
    attended = jnp.dot(context_b, merger, preferred_element_type=jnp.float32) + mergebias.astype(jnp.float32)
    preact = jnp.dot(normed_two, expand, preferred_element_type=jnp.float32) + expandbias.astype(jnp.float32)
    activ, slope = gelu_pair(preact)
    activ_b = activ.astype(jnp.bfloat16)
    mixed = jnp.dot(activ_b, contract, preferred_element_type=jnp.float32) + contractbias.astype(jnp.float32)
    output_row = (hidden_f + attended + mixed).astype(jnp.bfloat16)
    upstream = cotangent_row.astype(jnp.float32)
    outbias_grad = lax.optimization_barrier(jnp.sum(upstream, axis=0))
    merger_grad = jnp.dot(context_b.T, cotangent_row, preferred_element_type=jnp.float32)
    contract_grad = jnp.dot(activ_b.T, cotangent_row, preferred_element_type=jnp.float32)
    dpreact = jnp.dot(cotangent_row, contract.T, preferred_element_type=jnp.float32) * slope
    expandbias_grad = lax.optimization_barrier(jnp.sum(dpreact, axis=0))
    dpreact_b = dpreact.astype(jnp.bfloat16)
    expand_grad = jnp.dot(normed_two.T, dpreact_b, preferred_element_type=jnp.float32)
    dnormed_two = jnp.dot(dpreact_b, expand.T, preferred_element_type=jnp.float32)
    dcontext = jnp.dot(cotangent_row, merger.T, preferred_element_type=jnp.float32).astype(jnp.bfloat16).reshape(length, HEADS, head_dim)
    attention_back = jnp.where(allowed[None], jnp.exp(scores - logsum), 0.0)
    dattention = jnp.einsum('qhd,khd->hqk', dcontext.astype(jnp.float32), values.astype(jnp.float32))
    delta = lax.optimization_barrier(jnp.sum(dcontext.astype(jnp.float32) * context, axis=-1))
    dscores = (attention_back * (dattention - jnp.transpose(delta)[:, :, None]) * scale).astype(jnp.bfloat16)
    dqueries = jnp.einsum('hqk,khd->qhd', dscores.astype(jnp.float32), keys.astype(jnp.float32))
    dkeys = jnp.einsum('hqk,qhd->khd', dscores.astype(jnp.float32), queries.astype(jnp.float32))
    dvalues = jnp.einsum('hqk,qhd->khd', attention_back.astype(jnp.bfloat16).astype(jnp.float32), dcontext.astype(jnp.float32))
    dprojected = jnp.concatenate([unrotate(dqueries, cosine, sine).reshape(length, width), unrotate(dkeys, cosine, sine).reshape(length, width), dvalues.reshape(length, width)], axis=1)
    packbias_grad = lax.optimization_barrier(jnp.sum(dprojected, axis=0))
    dprojected_b = dprojected.astype(jnp.bfloat16)
    packed_grad = jnp.dot(normed_one.T, dprojected_b, preferred_element_type=jnp.float32)
    dnormed_one = jnp.dot(dprojected_b, packed.T, preferred_element_type=jnp.float32)
    back_one, firstgain_grad, firstshift_grad = norm_back(dnormed_one, normal_one, rscale_one, gain_one)
    back_two, secondgain_grad, secondshift_grad = norm_back(dnormed_two, normal_two, rscale_two, gain_two)
    backflow_row = upstream + back_one + back_two
    grads = (packed_grad, packbias_grad, merger_grad, outbias_grad, expand_grad, expandbias_grad, contract_grad, outbias_grad, firstgain_grad, firstshift_grad, secondgain_grad, secondshift_grad)
    return (output_row, backflow_row, grads)

def reference(hidden, cotangent, segments, packed, packbias, merger, mergebias, expand, expandbias, contract, contractbias, firstgain, firstshift, secondgain, secondshift):
    params = (packed, packbias, merger, mergebias, expand, expandbias, contract, contractbias, firstgain, firstshift, secondgain, secondshift)

    def advance(carry, row):
        hidden_row, cotangent_row, segment_row = row
        output_row, backflow_row, grads = row_pass(hidden_row, cotangent_row, segment_row, *params)
        carry = tuple((left + right for left, right in zip(carry, grads)))
        return (carry, (output_row, backflow_row))
    zeros = tuple((jnp.zeros(param.shape, jnp.float32) for param in params))
    totals, (output, backflow) = lax.scan(advance, zeros, (hidden, cotangent, segments))
    return (output, backflow, totals[0], totals[1], totals[2], totals[3], totals[4], totals[5], totals[6], totals[7], totals[8], totals[9], totals[10], totals[11])
```

```python
import math

import jax
import jax.numpy as jnp
from jax import lax
from jax.sharding import PartitionSpec as P

HEADS = 16
ROT = 16


epsilon = 1e-05
rotary_base = 10000.0


BF = jnp.bfloat16
F32 = jnp.float32


def normalise(values_in):
    centre = values_in - jnp.mean(values_in, axis=-1, keepdims=True)
    rscale = lax.rsqrt(jnp.mean(centre * centre, axis=-1, keepdims=True) + epsilon)
    return (centre * rscale, rscale)


def rotary_tables(position):
    half_rot = ROT // 2
    frequency = rotary_base ** (-(jnp.arange(half_rot, dtype=jnp.float32) * 2.0) / ROT)
    angles = position.astype(jnp.float32)[:, None] * frequency[None, :]
    cosine = jnp.concatenate([jnp.cos(angles), jnp.cos(angles)], axis=1)[:, None, :]
    sine = jnp.concatenate([jnp.sin(angles), jnp.sin(angles)], axis=1)[:, None, :]
    return (cosine, sine)


def rotate(tensor, cosine, sine):
    half_rot = ROT // 2
    front = tensor[..., :ROT]
    turned = jnp.concatenate([-front[..., half_rot:], front[..., :half_rot]], axis=-1)
    return jnp.concatenate([front * cosine + turned * sine, tensor[..., ROT:]], axis=-1)


def unrotate(tensor, cosine, sine):
    half_rot = ROT // 2
    front = tensor[..., :ROT]
    moved = front * sine
    turned = jnp.concatenate([moved[..., half_rot:], -moved[..., :half_rot]], axis=-1)
    return jnp.concatenate([front * cosine + turned, tensor[..., ROT:]], axis=-1)


def gelu_pair(preact):
    cumulative = 0.5 * (1.0 + jax.scipy.special.erf(preact / math.sqrt(2.0)))
    density = jnp.exp(-0.5 * preact * preact) / math.sqrt(2.0 * math.pi)
    return (preact * cumulative, cumulative + preact * density)


def attention_pass(queries, keys_all, values_all, allowed, scale):
    scores = (
        jnp.einsum("qhd,khd->hqk", queries, keys_all, preferred_element_type=jnp.float32) * scale
    )
    scores = jnp.where(allowed[None], scores, -1e30)
    row_max = jnp.max(scores, axis=-1, keepdims=True)
    unscaled = jnp.where(allowed[None], jnp.exp(scores - row_max), 0.0)
    row_total = jnp.sum(unscaled, axis=-1, keepdims=True)
    logsum = row_max + jnp.log(row_total)
    attention = (unscaled / row_total).astype(jnp.bfloat16)
    context = jnp.einsum("hqk,khd->qhd", attention, values_all, preferred_element_type=jnp.float32)
    return (context, logsum)


def attention_back_pass(queries, keys_all, values_all, allowed, scale, logsum, context, dcontext):
    scores_again = (
        jnp.einsum("qhd,khd->hqk", queries, keys_all, preferred_element_type=jnp.float32) * scale
    )
    scores_again = jnp.where(allowed[None], scores_again, -1e30)
    attention_back = jnp.where(allowed[None], jnp.exp(scores_again - logsum), 0.0)
    dattention = jnp.einsum(
        "qhd,khd->hqk", dcontext, values_all, preferred_element_type=jnp.float32
    )
    delta = jnp.sum(dcontext.astype(jnp.float32) * context, axis=-1)
    dscores = (attention_back * (dattention - jnp.transpose(delta)[:, :, None]) * scale).astype(
        jnp.bfloat16
    )
    dqueries = jnp.einsum("hqk,khd->qhd", dscores, keys_all, preferred_element_type=jnp.float32)
    dkeys = jnp.einsum("hqk,qhd->khd", dscores, queries, preferred_element_type=jnp.float32)
    dvalues = jnp.einsum(
        "hqk,qhd->khd",
        attention_back.astype(jnp.bfloat16),
        dcontext,
        preferred_element_type=jnp.float32,
    )
    return (dqueries, dkeys, dvalues)


def spread(value, axis, partners):
    size = lax.axis_size(axis)
    return [value] + [
        lax.ppermute(value, axis, [(i, partner(i, size)) for i in range(size)])
        for partner in partners
    ]


def ring_gather(value, axis):
    size = lax.axis_size(axis)
    return spread(value, axis, [lambda i, n, k=k: (i + k) % n for k in range(1, size)])


def ring_scatter(blocks, axis):
    size = lax.axis_size(axis)
    total = blocks[0].astype(F32)
    for k in range(1, size):
        total = total + lax.ppermute(
            blocks[k], axis, [(i, (i - k) % size) for i in range(size)]
        ).astype(F32)
    return total


def core_swap(value):
    size = lax.axis_size("rep")
    return lax.ppermute(value, "rep", [(i, i ^ 1) for i in range(size)])


def chip_move(value, m):
    size = lax.axis_size("rep")
    return lax.ppermute(value, "rep", [(i, i ^ (2 * m)) for i in range(size)])


def rep_scatter(grad):
    me = lax.axis_index("rep")
    core, chip = me % 2, me // 2
    chips = grad.shape[1]
    kept = lax.dynamic_index_in_dim(grad, core, 0, keepdims=False)
    sent = lax.dynamic_index_in_dim(grad, 1 - core, 0, keepdims=False)
    half = (kept.astype(F32) + core_swap(sent).astype(F32)).astype(BF)
    total = lax.dynamic_index_in_dim(half, chip, 0, keepdims=False).astype(F32)
    for m in range(1, chips):
        piece = lax.dynamic_index_in_dim(half, chip ^ m, 0, keepdims=False)
        total = total + chip_move(piece, m).astype(F32)
    return total.astype(BF)


def untangle(stack, index):
    count = stack.shape[0]
    step = 1
    while step < count:
        view = stack.reshape((count // (2 * step), 2, step) + stack.shape[1:])
        turned = view[:, ::-1]
        view = jnp.where((index // step) % 2 == 1, turned, view)
        stack = view.reshape(stack.shape)
        step *= 2
    return stack


def rep_gather(block):
    me = lax.axis_index("rep")
    chips = lax.axis_size("rep") // 2
    stack = jnp.stack([block] + [chip_move(block, m) for m in range(1, chips)])
    other = core_swap(stack)
    both = untangle(jnp.stack([stack, other]), me % 2)
    return jnp.moveaxis(untangle(jnp.moveaxis(both, 1, 0), me // 2), 0, 1)


def tensor_plan(
    hidden,
    cotangent,
    segments,
    packed,
    packbias,
    merger,
    mergebias,
    expand,
    expandbias,
    contract,
    contractbias,
    firstgain,
    firstshift,
    secondgain,
    secondshift,
):
    shards = lax.axis_size("shard")
    reps = lax.axis_size("rep")
    chips = reps // 2
    shard_index = lax.axis_index("shard")
    rep_index = lax.axis_index("rep")
    tokens = hidden.shape[1]
    width = hidden.shape[2]
    param_rows = packed.shape[0]
    hidden_units = expand.shape[1]
    own_width = width // shards
    own_units = hidden_units // shards
    own_heads = HEADS // shards
    head_dim = width // HEADS
    scale = 1.0 / math.sqrt(head_dim)
    length = tokens * shards
    slab = param_rows // reps
    mixed_width = 3 * own_width + own_units

    place = (rep_index % 2) * chips + rep_index // 2
    packed_rows = lax.dynamic_slice_in_dim(packed, place * slab, slab, 0)
    expand_rows = lax.dynamic_slice_in_dim(expand, place * slab, slab, 0)
    outgoing = jnp.concatenate(
        [
            packed_rows.reshape(slab, 3, shards, own_width)
            .transpose(2, 0, 1, 3)
            .reshape(shards, slab, 3 * own_width),
            expand_rows.reshape(slab, shards, own_units).transpose(1, 0, 2),
        ],
        axis=2,
    )
    incoming = lax.all_to_all(outgoing, "shard", split_axis=0, concat_axis=0, tiled=True)

    small = jnp.concatenate(
        [
            segments[0].astype(BF),
            mergebias,
            contractbias,
            firstgain,
            firstshift,
            secondgain,
            secondshift,
            packbias,
        ]
    )
    small_rows = -(-small.shape[0] // width)
    small = jnp.pad(small, (0, small_rows * width - small.shape[0])).reshape(small_rows, width)
    gathered = ring_gather(jnp.concatenate([hidden[0], small]), "shard")
    row_hidden = jnp.concatenate([block[:tokens] for block in gathered])
    smalls = jnp.stack([block[tokens:].reshape(-1) for block in gathered])
    row_segments = smalls[:, :tokens].reshape(length)
    order = (shard_index - jnp.arange(shards)) % shards
    smalls = jnp.zeros_like(smalls).at[order].set(smalls)
    vectors = smalls[:, tokens : tokens + 6 * own_width].reshape(shards, 6, own_width)
    vectors = vectors.transpose(1, 0, 2).reshape(6, width).astype(F32)
    outbias = vectors[0] + vectors[1]
    gain_one, shift_one, gain_two, shift_two = vectors[2], vectors[3], vectors[4], vectors[5]
    packbias_full = smalls[:, tokens + 6 * own_width : tokens + 9 * own_width].reshape(3 * width)
    upstream_b = jnp.concatenate(ring_gather(cotangent[0], "shard"))

    columns = rep_gather(incoming)
    columns = columns.transpose(2, 0, 1, 3, 4).reshape(width, mixed_width)
    packed_cols = columns[:, : 3 * own_width]
    expand_cols = columns[:, 3 * own_width :]

    indices = (order[:, None] * tokens + jnp.arange(tokens)[None, :]).reshape(length)
    starts = jnp.sum((row_segments[None, :] < row_segments[:, None]).astype(jnp.int32), axis=1)
    cosine, sine = rotary_tables(indices - starts)
    allowed = (row_segments[:, None] == row_segments[None, :]) & (
        indices[None, :] <= indices[:, None]
    )
    normal, rscale = normalise(row_hidden.astype(F32))
    normed_one = (normal * gain_one + shift_one).astype(BF)
    normed_two = (normal * gain_two + shift_two).astype(BF)
    packbias_own = lax.dynamic_slice_in_dim(
        packbias_full.reshape(3, shards, own_width), shard_index, 1, 1
    ).reshape(3 * own_width)
    projected = jnp.dot(normed_one, packed_cols, preferred_element_type=F32) + packbias_own.astype(
        F32
    )
    queries = rotate(
        projected[:, :own_width].reshape(length, own_heads, head_dim), cosine, sine
    ).astype(BF)
    keys_all = rotate(
        projected[:, own_width : 2 * own_width].reshape(length, own_heads, head_dim), cosine, sine
    ).astype(BF)
    values_all = projected[:, 2 * own_width :].reshape(length, own_heads, head_dim).astype(BF)
    preact = jnp.dot(normed_two, expand_cols, preferred_element_type=F32) + expandbias.astype(F32)
    activ, slope = gelu_pair(preact)
    activ_b = activ.astype(BF)
    context, logsum = attention_pass(queries, keys_all, values_all, allowed, scale)
    context_b = context.reshape(length, own_width).astype(BF)
    partial_value = (
        jnp.dot(context_b, merger, preferred_element_type=F32)
        + jnp.dot(activ_b, contract, preferred_element_type=F32)
    ).astype(BF)
    branches = ring_scatter(
        [partial_value[k * tokens : (k + 1) * tokens] for k in range(shards)], "shard"
    )
    output = (hidden[0].astype(F32) + branches + outbias).astype(BF)

    outbias_full = jnp.sum(upstream_b.astype(F32), axis=0)
    contract_grad = jnp.dot(activ_b.T, upstream_b, preferred_element_type=F32).astype(BF)
    merger_grad = jnp.dot(context_b.T, upstream_b, preferred_element_type=F32).astype(BF)
    dpreact = jnp.dot(upstream_b, contract.T, preferred_element_type=F32) * slope
    expandbias_grad = jnp.sum(dpreact, axis=0)
    dpreact_b = dpreact.astype(BF)
    expand_grad = jnp.dot(normed_two.T, dpreact_b, preferred_element_type=F32).astype(BF)

    contract_sum = rep_gather(rep_scatter(contract_grad.reshape(2, chips, -1, width)))
    merger_sum = rep_gather(rep_scatter(merger_grad.reshape(2, chips, -1, width)))

    def column_total(grad, units):
        blocks = grad.reshape(shards, 2, chips, slab, units).transpose(1, 2, 0, 3, 4)
        mine = rep_scatter(blocks)
        mine = lax.all_to_all(mine, "shard", split_axis=0, concat_axis=0, tiled=True)
        return rep_gather(mine)

    expand_sum = column_total(expand_grad, own_units)
    expand_sum = expand_sum.transpose(0, 1, 3, 2, 4).reshape(param_rows, hidden_units)

    dcontext = (
        jnp.dot(upstream_b, merger.T, preferred_element_type=F32)
        .astype(BF)
        .reshape(length, own_heads, head_dim)
    )
    dqueries, dkeys, dvalues = attention_back_pass(
        queries, keys_all, values_all, allowed, scale, logsum, context, dcontext
    )
    dprojected = jnp.concatenate(
        [
            unrotate(dqueries, cosine, sine).reshape(length, own_width),
            unrotate(dkeys, cosine, sine).reshape(length, own_width),
            dvalues.reshape(length, own_width),
        ],
        axis=1,
    )
    packbias_grad = jnp.sum(dprojected, axis=0)
    dprojected_b = dprojected.astype(BF)
    packed_grad = jnp.dot(normed_one.T, dprojected_b, preferred_element_type=F32).astype(BF)
    packed_sum = column_total(packed_grad, 3 * own_width)
    packed_sum = (
        packed_sum.reshape(2, chips, shards, slab, 3, own_width)
        .transpose(0, 1, 3, 4, 2, 5)
        .reshape(param_rows, 3 * width)
    )

    dnormed_one = jnp.dot(dprojected_b, packed_cols.T, preferred_element_type=F32)
    dnormed_two = jnp.dot(dpreact_b, expand_cols.T, preferred_element_type=F32)
    scaled = (dnormed_one * gain_one + dnormed_two * gain_two).astype(BF)
    scaled_own = ring_scatter(
        [scaled[k * tokens : (k + 1) * tokens] for k in range(shards)], "shard"
    )
    normal_own, rscale_own = normal[:tokens], rscale[:tokens]
    back = rscale_own * (
        scaled_own
        - jnp.mean(scaled_own, axis=-1, keepdims=True)
        - normal_own * jnp.mean(scaled_own * normal_own, axis=-1, keepdims=True)
    )
    backflow = cotangent[0].astype(F32) + back

    selector = (jnp.arange(shards, dtype=jnp.int32) == shard_index).astype(F32)
    placed = (selector[None, :, None] * packbias_grad.reshape(3, 1, own_width)).reshape(
        shards, 3 * own_width
    )
    parts = [
        jnp.sum(dnormed_one * normal, axis=0),
        jnp.sum(dnormed_one, axis=0),
        jnp.sum(dnormed_two * normal, axis=0),
        jnp.sum(dnormed_two, axis=0),
    ]
    sent = jnp.concatenate([placed] + [part.reshape(shards, own_width) for part in parts], axis=1)
    got = lax.all_to_all(sent.astype(BF), "shard", split_axis=0, concat_axis=0, tiled=True)
    outbias_own = lax.dynamic_slice_in_dim(outbias_full, shard_index * own_width, own_width, 0)
    mine = jnp.concatenate([jnp.sum(got.astype(F32), axis=0), outbias_own, expandbias_grad])
    total = lax.psum(mine.astype(BF), "rep").astype(F32)
    cuts = [3 * own_width] + [3 * own_width + own_width * k for k in range(1, 6)]
    packbias_sum, gain_a, shift_a, gain_b, shift_b, outbias_sum, expandbias_sum = jnp.split(
        total, cuts
    )
    return (
        output[None],
        backflow[None],
        packed_sum.astype(F32),
        packbias_sum,
        merger_sum.reshape(own_width, width).astype(F32),
        outbias_sum,
        expand_sum.astype(F32),
        expandbias_sum,
        contract_sum.reshape(own_units, width).astype(F32),
        outbias_sum,
        gain_a,
        shift_a,
        gain_b,
        shift_b,
    )


def solution(mesh):
    placed = (
        P("rep", "shard", None),
        P("rep", "shard", None),
        P("rep", "shard"),
        P("shard", None),
        P("shard"),
        P("shard", None),
        P("shard"),
        P("shard", None),
        P("shard"),
        P("shard", None),
        P("shard"),
        P("shard"),
        P("shard"),
        P("shard"),
        P("shard"),
    )
    return jax.shard_map(
        tensor_plan,
        mesh=mesh,
        in_specs=placed,
        out_specs=(
            P("rep", "shard", None),
            P("rep", "shard", None),
            P("shard", None),
            P("shard"),
            P("shard", None),
            P("shard"),
            P("shard", None),
            P("shard"),
            P("shard", None),
            P("shard"),
            P("shard"),
            P("shard"),
            P("shard"),
            P("shard"),
        ),
        check_vma=False,
    )
```

```python
import functools
import math

import jax
import jax.numpy as jnp
from jax import lax
from jax.experimental import pallas as pl
from jax.experimental.pallas import tpu as pltpu
from jax.sharding import PartitionSpec as P

HEADS = 16
ROT = 16


epsilon = 1e-05
rotary_base = 10000.0


BF = jnp.bfloat16
F32 = jnp.float32


def normalise(values_in):
    centre = values_in - jnp.mean(values_in, axis=-1, keepdims=True)
    rscale = lax.rsqrt(jnp.mean(centre * centre, axis=-1, keepdims=True) + epsilon)
    return (centre * rscale, rscale)


def gelu_pair(preact):
    cumulative = 0.5 * (1.0 + jax.scipy.special.erf(preact / math.sqrt(2.0)))
    density = jnp.exp(-0.5 * preact * preact) / math.sqrt(2.0 * math.pi)
    return (preact * cumulative, cumulative + preact * density)


def spread(value, axis, partners):
    size = lax.axis_size(axis)
    return [value] + [
        lax.ppermute(value, axis, [(i, partner(i, size)) for i in range(size)])
        for partner in partners
    ]


def ring_gather(value, axis):
    size = lax.axis_size(axis)
    return spread(value, axis, [lambda i, n, k=k: (i + k) % n for k in range(1, size)])


def ring_scatter(blocks, axis):
    size = lax.axis_size(axis)
    total = blocks[0].astype(F32)
    for k in range(1, size):
        total = total + lax.ppermute(
            blocks[k], axis, [(i, (i - k) % size) for i in range(size)]
        ).astype(F32)
    return total


def core_swap(value):
    size = lax.axis_size("rep")
    return lax.ppermute(value, "rep", [(i, i ^ 1) for i in range(size)])


def chip_move(value, m):
    size = lax.axis_size("rep")
    return lax.ppermute(value, "rep", [(i, i ^ (2 * m)) for i in range(size)])


def rep_scatter_plain(grad):
    me = lax.axis_index("rep")
    core, chip = me % 2, me // 2
    chips = grad.shape[1]
    kept = lax.dynamic_index_in_dim(grad, core, 0, keepdims=False)
    sent = lax.dynamic_index_in_dim(grad, 1 - core, 0, keepdims=False)
    half = (kept.astype(F32) + core_swap(sent).astype(F32)).astype(BF)
    total = lax.dynamic_index_in_dim(half, chip, 0, keepdims=False).astype(F32)
    for m in range(1, chips):
        piece = lax.dynamic_index_in_dim(half, chip ^ m, 0, keepdims=False)
        total = total + chip_move(piece, m).astype(F32)
    return total.astype(BF)


def untangle(stack, index):
    count = stack.shape[0]
    step = 1
    while step < count:
        view = stack.reshape((count // (2 * step), 2, step) + stack.shape[1:])
        turned = view[:, ::-1]
        view = jnp.where((index // step) % 2 == 1, turned, view)
        stack = view.reshape(stack.shape)
        step *= 2
    return stack


def rep_gather_plain(block):
    me = lax.axis_index("rep")
    chips = lax.axis_size("rep") // 2
    stack = jnp.stack([block] + [chip_move(block, m) for m in range(1, chips)])
    other = core_swap(stack)
    both = untangle(jnp.stack([stack, other]), me % 2)
    return jnp.moveaxis(untangle(jnp.moveaxis(both, 1, 0), me // 2), 0, 1)


def chip_gather(block):
    chips = lax.axis_size("rep") // 2
    return [block] + [chip_move(block, m) for m in range(1, chips)]


def rep_scatter(where, tiled, grads):
    chips = grads[0].shape[1]
    if not tiled:
        return jnp.concatenate([rep_scatter_plain(grad) for grad in grads])
    core = lax.axis_index("rep") % 2
    halves = [
        core_swap(lax.dynamic_index_in_dim(grad, 1 - core, 0, keepdims=False)) for grad in grads
    ]
    pieces = split_sum(where, grads, halves)
    total = pieces[0].astype(F32)
    for m in range(1, chips):
        total = total + chip_move(pieces[m], m).astype(F32)
    return total.astype(BF)


def rep_gather(where, tiled, block, shapes, outs_of):
    if tiled:
        mine = chip_gather(block)
        return widen(where, mine, [core_swap(piece) for piece in mine], shapes, outs_of)
    every = rep_gather_plain(block)
    outs = []
    for shape, parts in zip(shapes, outs_of):
        out = jnp.zeros((every.shape[0], every.shape[1], parts[0][1], shape[1]), F32)
        for top, rows, left, cols, column in parts:
            piece = every[:, :, top : top + rows, left : left + cols].astype(F32)
            out = out.at[:, :, :, column : column + cols].set(piece)
        outs.append(out.reshape(shape))
    return outs


def lane_masks(shape):
    lane = lax.broadcasted_iota(jnp.int32, shape, 1) % (2 * ROT * 2)
    return lane < ROT // 2, (lane >= ROT // 2) & (lane < ROT)


def forward_kernel(
    blocks, heads_each, scale, normed, weights, bias, cosine, sine, aux, order, qkv, attn, ctx, ctx_b
):
    pair = pl.program_id(0)
    lanes = 128
    length = normed.shape[0]
    head_dim = lanes // heads_each

    @pl.when(pair == 0)
    def _():
        first, second = lane_masks((length, lanes))
        cos, sin = cosine[...], sine[...]
        ahead = jnp.where(first, -sin, 0.0)
        behind = jnp.where(second, sin, 0.0)
        for part in range(3 * blocks):
            cols = pl.ds(part * lanes, lanes)
            if part % 2 == 0 and part + 1 < 3 * blocks:
                wide = (
                    jnp.dot(
                        normed[...],
                        weights[:, pl.ds(part * lanes, 2 * lanes)],
                        preferred_element_type=F32,
                    )
                    + bias[0:1, pl.ds(part * lanes, 2 * lanes)]
                )
                value = wide[:, :lanes]
            elif part % 2 == 1:
                value = wide[:, lanes:]
            else:
                value = (
                    jnp.dot(normed[...], weights[:, cols], preferred_element_type=F32)
                    + bias[0:1, cols]
                )
            if part < 2 * blocks:
                value = (
                    value * cos
                    + pltpu.roll(value, lanes - ROT // 2, 1) * ahead
                    + pltpu.roll(value, ROT // 2, 1) * behind
                )
            qkv[part] = value.astype(BF)

    start, index = aux[:, 0:1], aux[:, 1:2]
    place = order[0:1, :]
    allowed = (place >= start) & (place <= index)
    query, key, value = qkv[pair], qkv[blocks + pair], qkv[2 * blocks + pair]
    out = []
    for h in range(heads_each):
        cut = slice(h * head_dim, (h + 1) * head_dim)
        scores = (
            lax.dot_general(
                query[:, cut], key[:, cut], (((1,), (1,)), ((), ())), preferred_element_type=F32
            )
            * scale
        )
        scores = jnp.where(allowed, scores, -1e30)
        raised = jnp.exp(scores - jnp.max(scores, axis=1, keepdims=True))
        share = raised / jnp.sum(raised, axis=1, keepdims=True)
        share = share.astype(BF)
        attn[h] = share
        out.append(jnp.dot(share, value[:, cut], preferred_element_type=F32))
    both = jnp.concatenate(out, axis=1)
    ctx[0] = both
    ctx_b[...] = both.astype(BF)


def attention_forward(normed, columns, bias, cosine, sine, aux, order, own_width, scale, head_dim):
    length, width = normed.shape
    blocks = own_width // 128
    each = 128 // head_dim
    whole = lambda shape: pl.BlockSpec(shape, lambda p: (0,) * len(shape))
    return pl.pallas_call(
        functools.partial(forward_kernel, blocks, each, scale),
        grid=(blocks,),
        in_specs=[
            whole((length, width)),
            whole((width, 3 * own_width)),
            whole((1, 3 * own_width)),
            whole((length, 128)),
            whole((length, 128)),
            whole((length, 128)),
            whole((1, length)),
        ],
        out_specs=[
            whole((3 * blocks, length, 128)),
            pl.BlockSpec((each, length, length), lambda p: (p, 0, 0)),
            pl.BlockSpec((1, length, 128), lambda p: (p, 0, 0)),
            pl.BlockSpec((length, 128), lambda p: (0, p)),
        ],
        out_shape=[
            jax.ShapeDtypeStruct((3 * blocks, length, 128), BF),
            jax.ShapeDtypeStruct((each * blocks, length, length), BF),
            jax.ShapeDtypeStruct((blocks, length, 128), F32),
            jax.ShapeDtypeStruct((length, own_width), BF),
        ],
        name="attention_forward",
    )(normed, columns, bias, cosine, sine, aux, order)


def backward_kernel(
    blocks, heads_each, scale, cot, merger, qkv, attn, ctx, cosine, sine, dproj, dbias, dctx
):
    pair = pl.program_id(0)
    lanes = 128
    length = cot.shape[0]
    head_dim = lanes // heads_each

    @pl.when(pair == 0)
    def _():
        full = lax.dot_general(
            cot[...], merger[...], (((1,), (1,)), ((), ())), preferred_element_type=F32
        ).astype(BF)
        for b in range(blocks):
            dctx[b] = full[:, b * lanes : (b + 1) * lanes]
        dbias[...] = jnp.zeros_like(dbias)

    query, key, value = qkv[pair], qkv[blocks + pair], qkv[2 * blocks + pair]
    upward = dctx[pair]
    product = upward.astype(F32) * ctx[0]
    grads = ([], [], [])
    for h in range(heads_each):
        cut = slice(h * head_dim, (h + 1) * head_dim)
        share = attn[h]
        up = upward[:, cut]
        delta = jnp.sum(product[:, cut], axis=1, keepdims=True)
        dshare = lax.dot_general(
            up, value[:, cut], (((1,), (1,)), ((), ())), preferred_element_type=F32
        )
        dscore = (share.astype(F32) * (dshare - delta) * scale).astype(BF)
        grads[0].append(jnp.dot(dscore, key[:, cut], preferred_element_type=F32))
        over = (((0,), (0,)), ((), ()))
        grads[1].append(
            lax.dot_general(dscore, query[:, cut], over, preferred_element_type=F32)
        )
        grads[2].append(lax.dot_general(share, up, over, preferred_element_type=F32))
    first, second = lane_masks((length, lanes))
    cos, sin = cosine[...], sine[...]
    for part in range(3):
        grad = jnp.concatenate(grads[part], axis=1)
        if part < 2:
            moved = grad * sin
            grad = (
                grad * cos
                + jnp.where(first, pltpu.roll(moved, lanes - ROT // 2, 1), 0.0)
                - jnp.where(second, pltpu.roll(moved, ROT // 2, 1), 0.0)
            )
        cols = pl.ds(pl.multiple_of((part * blocks + pair) * lanes, lanes), lanes)
        dbias[0:1, cols] = jnp.sum(grad, axis=0, keepdims=True)
        dproj[:, cols] = grad.astype(BF)


def attention_backward(cot, merger, qkv, attn, ctx, cosine, sine, scale, head_dim):
    length, width = cot.shape
    own_width = merger.shape[0]
    blocks = own_width // 128
    each = 128 // head_dim
    whole = lambda shape: pl.BlockSpec(shape, lambda p: (0,) * len(shape))
    return pl.pallas_call(
        functools.partial(backward_kernel, blocks, each, scale),
        grid=(blocks,),
        in_specs=[
            whole((length, width)),
            whole((own_width, width)),
            whole((3 * blocks, length, 128)),
            pl.BlockSpec((each, length, length), lambda p: (p, 0, 0)),
            pl.BlockSpec((1, length, 128), lambda p: (p, 0, 0)),
            whole((length, 128)),
            whole((length, 128)),
        ],
        out_specs=[whole((length, 3 * own_width)), whole((8, 3 * own_width))],
        out_shape=[
            jax.ShapeDtypeStruct((length, 3 * own_width), BF),
            jax.ShapeDtypeStruct((8, 3 * own_width), F32),
        ],
        scratch_shapes=[pltpu.VMEM((blocks, length, 128), BF)],
        name="attention_backward",
    )(cot, merger, qkv, attn, ctx, cosine, sine)


def split_kernel(count, chips, where_ref, *refs):
    grads, halves, pieces = refs[:count], refs[count : 2 * count], refs[2 * count :]
    core, chip = where_ref[0], where_ref[1]
    for m in range(chips):
        at = 0
        for grad, half in zip(grads, halves):
            rows = grad.shape[2]
            pieces[m][at : at + rows] = (
                grad[core, chip ^ m].astype(F32) + half[chip ^ m].astype(F32)
            ).astype(BF)
            at += rows


def split_sum(where, grads, halves):
    chips = grads[0].shape[1]
    rows = sum(grad.shape[2] for grad in grads)
    cols = grads[0].shape[3]
    vmem = pl.BlockSpec(memory_space=pltpu.VMEM)
    return pl.pallas_call(
        functools.partial(split_kernel, len(grads), chips),
        in_specs=[pl.BlockSpec(memory_space=pltpu.SMEM)] + [vmem] * (2 * len(grads)),
        out_specs=[vmem] * chips,
        out_shape=[jax.ShapeDtypeStruct((rows, cols), BF)] * chips,
        name="split_sum",
    )(where, *grads, *halves)


def widen_kernel(count, outs_of, where_ref, *refs):
    pieces = refs[:count]
    outs = refs[count : count + len(outs_of)]
    buffers = refs[count + len(outs_of) : -1]
    sem = refs[-1]
    core, chip = where_ref[0], where_ref[1]
    chips = count // 2
    copies = []
    for i in range(count):
        m, swapped = i % chips, i // chips
        block = ((1 - core) if swapped else core) * chips + (chip ^ m)
        for which, parts in enumerate(outs_of):
            rows = parts[0][1]
            for top, _, left, cols, column in parts:
                buffers[which][i, :, column : column + cols] = pieces[i][
                    top : top + rows, left : left + cols
                ].astype(F32)
            row = pl.multiple_of(block * rows, rows)
            copy = pltpu.make_async_copy(
                buffers[which].at[i],
                outs[which].at[pl.ds(row, rows), :],
                sem.at[i * len(outs_of) + which],
            )
            copy.start()
            copies.append(copy)
    for copy in copies:
        copy.wait()


def widen(where, mine, other, shapes, outs_of):
    pieces = list(mine) + list(other)
    vmem = pl.BlockSpec(memory_space=pltpu.VMEM)
    return pl.pallas_call(
        functools.partial(widen_kernel, len(pieces), outs_of),
        in_specs=[pl.BlockSpec(memory_space=pltpu.SMEM)] + [vmem] * len(pieces),
        out_specs=[pl.BlockSpec(memory_space=pl.ANY)] * len(shapes),
        out_shape=[jax.ShapeDtypeStruct(shape, F32) for shape in shapes],
        scratch_shapes=[
            pltpu.VMEM((len(pieces), parts[0][1], shape[1]), F32)
            for parts, shape in zip(outs_of, shapes)
        ]
        + [pltpu.SemaphoreType.DMA((len(pieces) * len(shapes),))],
        name="widen",
    )(where, *pieces)


def assemble_kernel(count, groups, cuts, where_ref, *refs):
    pieces, outs = refs[:count], refs[count:]
    core, chip = where_ref[0], where_ref[1]
    chips = count // 2
    slab = pieces[0].shape[0] // groups
    for i in range(count):
        m, swapped = i % chips, i // chips
        block = ((1 - core) if swapped else core) * chips + (chip ^ m)
        for group in range(groups):
            row = pl.multiple_of(group * count * slab + block * slab, slab)
            for out, (left, right) in zip(outs, cuts):
                out[pl.ds(row, slab), :] = pieces[i][group * slab : (group + 1) * slab, left:right]


def assemble(where, mine, other, groups, cuts):
    pieces = list(mine) + list(other)
    rows = pieces[0].shape[0] * len(pieces)
    vmem = pl.BlockSpec(memory_space=pltpu.VMEM)
    return pl.pallas_call(
        functools.partial(assemble_kernel, len(pieces), groups, cuts),
        in_specs=[pl.BlockSpec(memory_space=pltpu.SMEM)] + [vmem] * len(pieces),
        out_specs=[vmem] * len(cuts),
        out_shape=[jax.ShapeDtypeStruct((rows, right - left), BF) for left, right in cuts],
        name="assemble",
    )(where, *pieces)


def norms_kernel(tokens, vectors, *refs):
    blocks, (one, two, normal_out) = refs[:-3], refs[-3:]
    for k, block in enumerate(blocks):
        rows = pl.ds(k * tokens, tokens)
        normal, _ = normalise(block[0:tokens, :].astype(F32))
        normal_out[rows, :] = normal
        one[rows, :] = (normal * vectors[2:3, :] + vectors[3:4, :]).astype(BF)
        two[rows, :] = (normal * vectors[4:5, :] + vectors[5:6, :]).astype(BF)


def norms(vectors, blocks, tokens):
    width = blocks[0].shape[1]
    length = tokens * len(blocks)
    vmem = pl.BlockSpec(memory_space=pltpu.VMEM)
    return pl.pallas_call(
        functools.partial(norms_kernel, tokens),
        in_specs=[vmem] * (1 + len(blocks)),
        out_specs=[vmem] * 3,
        out_shape=[
            jax.ShapeDtypeStruct((length, width), BF),
            jax.ShapeDtypeStruct((length, width), BF),
            jax.ShapeDtypeStruct((length, width), F32),
        ],
        name="norms",
    )(vectors, *blocks)


def tensor_plan(
    hidden,
    cotangent,
    segments,
    packed,
    packbias,
    merger,
    mergebias,
    expand,
    expandbias,
    contract,
    contractbias,
    firstgain,
    firstshift,
    secondgain,
    secondshift,
):
    shards = lax.axis_size("shard")
    reps = lax.axis_size("rep")
    chips = reps // 2
    shard_index = lax.axis_index("shard")
    rep_index = lax.axis_index("rep")
    tokens = hidden.shape[1]
    width = hidden.shape[2]
    param_rows = packed.shape[0]
    hidden_units = expand.shape[1]
    own_width = width // shards
    own_units = hidden_units // shards
    head_dim = width // HEADS
    scale = 1.0 / math.sqrt(head_dim)
    length = tokens * shards
    slab = param_rows // reps
    tiled = slab % 16 == 0
    core, chip = rep_index % 2, rep_index // 2
    where = jnp.where(jnp.arange(2) == 0, core, chip).astype(jnp.int32)

    place = core * chips + chip
    packed_rows = lax.dynamic_slice_in_dim(packed, place * slab, slab, 0)
    expand_rows = lax.dynamic_slice_in_dim(expand, place * slab, slab, 0)
    outgoing = jnp.concatenate(
        [
            packed_rows.reshape(slab, 3, shards, own_width)
            .transpose(2, 0, 1, 3)
            .reshape(shards, slab, 3 * own_width),
            expand_rows.reshape(slab, shards, own_units).transpose(1, 0, 2),
        ],
        axis=2,
    )
    with jax.named_scope("weights_z"):
        incoming = lax.all_to_all(outgoing, "shard", split_axis=0, concat_axis=0, tiled=True)

    def as_row(vector):
        return jnp.pad(vector.astype(BF), (0, width - vector.shape[0]))

    small = jnp.stack(
        [
            as_row(vector)
            for vector in (
                mergebias,
                contractbias,
                firstgain,
                firstshift,
                secondgain,
                secondshift,
                packbias,
                segments[0],
            )
        ]
    )
    with jax.named_scope("rows_z"):
        gathered = ring_gather(jnp.concatenate([hidden[0], small]), "shard")
    smalls = jnp.stack([block[tokens:] for block in gathered])
    row_segments = smalls[:, 7, :tokens].reshape(length).astype(jnp.int32)
    order = (shard_index - jnp.arange(shards)) % shards
    sorter = (jnp.arange(shards)[:, None] == order[None, :]).astype(BF)
    ordered = jnp.dot(
        sorter, smalls.reshape(shards, 8 * width), preferred_element_type=F32
    ).reshape(shards, 8, width)
    vectors = ordered[:, :, :own_width].transpose(1, 0, 2).reshape(8, width)
    packbias_full = ordered[:, 6, : 3 * own_width].reshape(3 * width)
    packbias_own = lax.dynamic_slice_in_dim(
        packbias_full.reshape(3, shards, own_width), shard_index, 1, 1
    ).reshape(1, 3 * own_width)
    own_cot, _ = lax.optimization_barrier((cotangent[0], gathered[-1]))
    with jax.named_scope("cot_z"):
        upstream_b = jnp.concatenate(ring_gather(own_cot, "shard"))

    with jax.named_scope("weights_xy"):
        if tiled:
            block = incoming.reshape(shards * slab, -1)
            mine = chip_gather(block)
            other = [core_swap(piece) for piece in mine]
            packed_cols, expand_cols = assemble(
                where,
                mine,
                other,
                shards,
                ((0, 3 * own_width), (3 * own_width, 3 * own_width + own_units)),
            )
        else:
            columns = rep_gather_plain(incoming)
            columns = columns.transpose(2, 0, 1, 3, 4).reshape(width, -1)
            packed_cols = columns[:, : 3 * own_width]
            expand_cols = columns[:, 3 * own_width :]

    indices = (order[:, None] * tokens + jnp.arange(tokens)[None, :]).reshape(length)
    starts = jnp.sum((row_segments[None, :] < row_segments[:, None]).astype(jnp.int32), axis=1)
    lane = jnp.arange(128, dtype=jnp.int32)
    within = lane % head_dim
    frequency = jnp.where(
        within < ROT,
        rotary_base ** (-((within % (ROT // 2)).astype(F32) * 2.0) / ROT),
        0.0,
    )
    angles = (indices - starts).astype(F32)[:, None] * frequency[None, :]
    cosine, sine = jnp.cos(angles), jnp.sin(angles)
    aux = jnp.where((lane == 0)[None, :], starts[:, None], indices[:, None])

    normed_one, normed_two, normal = norms(vectors, gathered, tokens)
    qkv, attn, context, context_b = attention_forward(
        normed_one,
        packed_cols,
        packbias_own,
        cosine,
        sine,
        aux,
        indices[None, :],
        own_width,
        scale,
        head_dim,
    )
    preact = jnp.dot(normed_two, expand_cols, preferred_element_type=F32) + expandbias.astype(F32)
    activ, slope = gelu_pair(preact)
    activ_b = activ.astype(BF)
    partial_value = (
        jnp.dot(context_b, merger, preferred_element_type=F32)
        + jnp.dot(activ_b, contract, preferred_element_type=F32)
    ).astype(BF)
    with jax.named_scope("out_z"):
        branches = ring_scatter(
            [partial_value[k * tokens : (k + 1) * tokens] for k in range(shards)], "shard"
        )
    output = (hidden[0].astype(F32) + branches + (vectors[0] + vectors[1])).astype(BF)

    dpreact = jnp.dot(upstream_b, contract.T, preferred_element_type=F32) * slope
    expandbias_grad = jnp.sum(dpreact, axis=0)
    dpreact_b = dpreact.astype(BF)
    expand_grad = jnp.dot(normed_two.T, dpreact_b, preferred_element_type=F32).astype(BF)
    contract_grad = jnp.dot(activ_b.T, upstream_b, preferred_element_type=F32).astype(BF)
    merger_grad = jnp.dot(context_b.T, upstream_b, preferred_element_type=F32).astype(BF)
    outbias_full = jnp.sum(upstream_b.astype(F32), axis=0)

    def column_blocks(grad):
        units = grad.shape[1]
        return (
            grad.reshape(shards, 2, chips, slab, units)
            .transpose(1, 2, 0, 3, 4)
            .reshape(2, chips, shards * slab, units)
        )

    def to_owners(block):
        units = block.shape[1]
        return lax.all_to_all(
            block.reshape(shards, slab, units), "shard", split_axis=0, concat_axis=0, tiled=True
        ).reshape(shards * slab, units)

    with jax.named_scope("expand_sum"):
        expand_mine = to_owners(rep_scatter(where, tiled, [column_blocks(expand_grad)]))
        expand_parts = tuple(
            (s * slab, slab, 0, own_units, s * own_units) for s in range(shards)
        )
        (expand_sum,) = rep_gather(
            where, tiled, expand_mine, ((param_rows, hidden_units),), (expand_parts,)
        )
    with jax.named_scope("contract_sum"):
        rows_a, rows_b = own_units // reps, own_width // reps
        contract_mine = rep_scatter(
            where,
            tiled,
            [
                contract_grad.reshape(2, chips, rows_a, width),
                merger_grad.reshape(2, chips, rows_b, width),
            ],
        )
        contract_sum, merger_sum = rep_gather(
            where,
            tiled,
            contract_mine,
            ((own_units, width), (own_width, width)),
            (((0, rows_a, 0, width, 0),), ((rows_a, rows_b, 0, width, 0),)),
        )

    dprojected_b, dbias = attention_backward(
        upstream_b, merger, qkv, attn, context, cosine, sine, scale, head_dim
    )
    packbias_grad = dbias[0]
    packed_grad = jnp.dot(normed_one.T, dprojected_b, preferred_element_type=F32).astype(BF)
    with jax.named_scope("packed_sum"):
        packed_mine = to_owners(rep_scatter(where, tiled, [column_blocks(packed_grad)]))
        packed_parts = tuple(
            (s * slab, slab, part * own_width, own_width, part * width + s * own_width)
            for s in range(shards)
            for part in range(3)
        )
        (packed_sum,) = rep_gather(
            where, tiled, packed_mine, ((param_rows, 3 * width),), (packed_parts,)
        )

    gain_one, gain_two = vectors[2], vectors[4]
    dnormed_one = jnp.dot(dprojected_b, packed_cols.T, preferred_element_type=F32)
    dnormed_two = jnp.dot(dpreact_b, expand_cols.T, preferred_element_type=F32)
    scaled = (dnormed_one * gain_one + dnormed_two * gain_two).astype(BF)
    with jax.named_scope("back_z"):
        scaled_own = ring_scatter(
            [scaled[k * tokens : (k + 1) * tokens] for k in range(shards)], "shard"
        )
    normal_own, rscale_own = normalise(hidden[0].astype(F32))
    back = rscale_own * (
        scaled_own
        - jnp.mean(scaled_own, axis=-1, keepdims=True)
        - normal_own * jnp.mean(scaled_own * normal_own, axis=-1, keepdims=True)
    )
    backflow = cotangent[0].astype(F32) + back

    selector = (jnp.arange(shards, dtype=jnp.int32) == shard_index).astype(F32)
    placed = (selector[None, :, None] * packbias_grad.reshape(3, 1, own_width)).reshape(
        shards, 3 * own_width
    )
    parts = [
        jnp.sum(dnormed_one * normal, axis=0),
        jnp.sum(dnormed_one, axis=0),
        jnp.sum(dnormed_two * normal, axis=0),
        jnp.sum(dnormed_two, axis=0),
    ]
    sent = jnp.concatenate([placed] + [part.reshape(shards, own_width) for part in parts], axis=1)
    with jax.named_scope("small_z"):
        got = lax.all_to_all(sent.astype(BF), "shard", split_axis=0, concat_axis=0, tiled=True)
    outbias_own = lax.dynamic_slice_in_dim(outbias_full, shard_index * own_width, own_width, 0)
    mine = jnp.concatenate([jnp.sum(got.astype(F32), axis=0), outbias_own, expandbias_grad])
    with jax.named_scope("small_rep"):
        total = lax.psum(mine.astype(BF), "rep").astype(F32)
    cuts = [3 * own_width] + [3 * own_width + own_width * k for k in range(1, 6)]
    packbias_sum, gain_a, shift_a, gain_b, shift_b, outbias_sum, expandbias_sum = jnp.split(
        total, cuts
    )
    return (
        output[None],
        backflow[None],
        packed_sum,
        packbias_sum,
        merger_sum,
        outbias_sum,
        expand_sum,
        expandbias_sum,
        contract_sum,
        outbias_sum,
        gain_a,
        shift_a,
        gain_b,
        shift_b,
    )


def solution(mesh):
    placed = (
        P("rep", "shard", None),
        P("rep", "shard", None),
        P("rep", "shard"),
        P("shard", None),
        P("shard"),
        P("shard", None),
        P("shard"),
        P("shard", None),
        P("shard"),
        P("shard", None),
        P("shard"),
        P("shard"),
        P("shard"),
        P("shard"),
        P("shard"),
    )
    return jax.shard_map(
        tensor_plan,
        mesh=mesh,
        in_specs=placed,
        out_specs=(
            P("rep", "shard", None),
            P("rep", "shard", None),
            P("shard", None),
            P("shard"),
            P("shard", None),
            P("shard"),
            P("shard", None),
            P("shard"),
            P("shard", None),
            P("shard"),
            P("shard"),
            P("shard"),
            P("shard"),
            P("shard"),
        ),
        check_vma=False,
    )
```
